256 devices in a mesh: rep: 4 (over y), blk: 64 (over x, z, core).
Axes of the slice: x: 4, y: 4, z: 8, core: 2. Of those that a mesh axis runs over, the one named last changes fastest.
Arguments:
- feats: bfloat16 [1024, 128, 256], P('blk'), may hold values from -6 to 6
- requests: int32 [64, 64], P('blk'), may hold values from 0 to 15
- tile_dest: int32 [64, 512], P('blk'), may hold values from 0 to 15, as said below
- tile_slot: int32 [64, 512], P('blk'), may hold values from 0 to 63, as said below
- tile_vals: bfloat16 [64, 512, 128, 128], P('blk', None, 'rep'), may hold values from -0.09375 to 0.09375
- w_self: bfloat16 [256, 256], replicated, may hold values from -0.375 to 0.375
- w_neigh: bfloat16 [256, 256], replicated, may hold values from -0.375 to 0.375
- bias: float32 [256], replicated, may hold values from -3 to 3
- cotangent: bfloat16 [1024, 128, 256], P('blk', 'rep'), may hold values from -6 to 6
Outputs:
- hidden: bfloat16 [1024, 128, 256], P('blk', 'rep')
- grad_self: float32 [256, 256], replicated
- grad_neigh: float32 [256, 256], replicated
- grad_bias: float32 [256], replicated
- feat_grad: bfloat16 [1024, 128, 256], P('blk', 'rep')
The draws below stay inside these ranges and needn't reach their ends.
Inputs may be any that keep to these rules, and one draw needn't show every extreme that they name: `tile_slot`: for each reader b, every owner index is named by exactly 8 of its tiles. `tile_dest`: no two tiles of one reader have both the same destination block and the same owner.
All inputs are finite; a program needn't handle non-finite values.
Results may differ from the reference program's by a relative error of at most 0.015.
Values may be sent and summed in bfloat16 or wider, within the bound.
A program may use at most 128 MiB of HBM per device.

```python
import math
import jax
import jax.numpy as jnp
from jax import lax

D = 256
TILE = 128
BLK_DEV = 16
OWNERS = 64
TILES = 512
NBLOCKS = 1024
NODES = 131072


def tile_pairs(key):
    base = jax.random.fold_in(key, 7)

    def one_reader(reader):
        reader_key = jax.random.fold_in(base, reader)
        order = jax.random.permutation(jax.random.fold_in(reader_key, 1), TILES)
        owner_ids = order % OWNERS
        ranking = order // OWNERS

        def one_owner(owner):
            return jax.random.permutation(jax.random.fold_in(reader_key, owner + 2), BLK_DEV)
        tables = jax.vmap(one_owner)(jnp.arange(OWNERS))
        dest_ids = tables[owner_ids, ranking]
        return (owner_ids.astype(jnp.int32), dest_ids.astype(jnp.int32))
    return jax.vmap(one_reader)(jnp.arange(OWNERS))


def draw_tile_slot(key, part):
    return tile_pairs(key)[0]


def draw_tile_dest(key, part):
    return tile_pairs(key)[1]


def set_ends(drawn, key, low, top_value):
    spot = [jax.random.randint(jax.random.fold_in(key, axis), (), 0, length) for axis, length in enumerate(drawn.shape)]
    widest = drawn.shape.index(max(drawn.shape))
    neighbour = spot[:widest] + [(spot[widest] + 1) % drawn.shape[widest]] + spot[widest + 1:]
    return drawn.at[tuple(spot)].set(low).at[tuple(neighbour)].set(top_value)


def block_scale(key, extent, shards, smallest, largest):
    def one(dim, blocks):
        draws = jax.random.uniform(jax.random.fold_in(jax.random.fold_in(key, 6), dim), (blocks,), jnp.float32, smallest / len(shards), largest / len(shards))
        return jnp.repeat(jnp.exp(draws), extent[dim] // blocks).reshape((-1,) + (1,) * (len(extent) - dim - 1))

    loudness = one(*shards[0])
    for cut in shards[1:]:
        loudness = loudness * one(*cut)
    return loudness


def noise(stream_key, extent, scale, limit, pieces=(), held_as=jnp.bfloat16):
    array = jax.random.normal(stream_key, extent, jnp.float32) * scale
    if len(pieces) > 0:
        array = block_scale(stream_key, extent, pieces, -0.22, 0.18) * array
    return jnp.clip(array, min=-limit, max=limit).astype(held_as)


def setup_inputs(seed: int = 0) -> dict:
    key_of = jax.random.split(jax.random.key(seed), 10)
    feats = noise(key_of[0], (NBLOCKS, TILE, D), 1.0, 6.0, ((0, 64),))
    requests = set_ends(jax.random.randint(key_of[1], (OWNERS, OWNERS), 0, BLK_DEV), jax.random.fold_in(key_of[1], 1), 0, BLK_DEV - 1).astype(jnp.int32)
    tile_dest = draw_tile_dest(jax.random.fold_in(key_of[9], 71), 0)
    tile_slot = draw_tile_slot(jax.random.fold_in(key_of[9], 71), 0)
    tile_vals = noise(key_of[4], (OWNERS, TILES, TILE, TILE), (OWNERS * TILE // 2) ** -0.5, 0.09375, ((0, 64), (2, 4)))
    w_self = noise(key_of[5], (D, D), D ** -0.5, 0.375)
    w_neigh = noise(key_of[6], (D, D), D ** -0.5, 0.375)
    bias = noise(key_of[7], (D,), 0.5, 3.0, (), jnp.float32)
    cotangent = noise(key_of[8], (NBLOCKS, TILE, D), 1.0, 6.0, ((0, 64), (1, 4)))
    return {"feats": feats, "requests": requests, "tile_dest": tile_dest, "tile_slot": tile_slot, "tile_vals": tile_vals, "w_self": w_self, "w_neigh": w_neigh, "bias": bias, "cotangent": cotangent}


def source_blocks(requests, tile_slot, reader):
    owner_ids = tile_slot[reader]
    return (owner_ids * BLK_DEV + requests[owner_ids, reader]).astype(jnp.int32)

def reference(feats, requests, tile_dest, tile_slot, tile_vals, w_self, w_neigh, bias, cotangent):

    def forward_one(reader):
        source_ids = source_blocks(requests, tile_slot, reader)
        sources = feats[source_ids].astype(jnp.float32)
        products = jnp.einsum('tij,tjd->tid', tile_vals[reader].astype(jnp.float32), sources)
        return jax.ops.segment_sum(products, tile_dest[reader], num_segments=BLK_DEV)
    readers = jnp.arange(OWNERS, dtype=jnp.int32)
    aggregate = lax.map(forward_one, readers)
    aggregate = aggregate.reshape(NODES, D).astype(jnp.bfloat16)
    feat_rows = feats.reshape(NODES, D)
    preact = jnp.dot(feat_rows, w_self, preferred_element_type=jnp.float32)
    preact = preact + jnp.dot(aggregate, w_neigh, preferred_element_type=jnp.float32) + bias
    hidden = jax.nn.silu(preact).astype(jnp.bfloat16)
    gating = jax.nn.sigmoid(preact)
    grad_pre = (cotangent.reshape(NODES, D).astype(jnp.float32) * gating * (1.0 + preact * (1.0 - gating))).astype(jnp.bfloat16)
    grad_scale = 1.0 / math.sqrt(NODES)
    grad_self = jnp.dot(feat_rows.T, grad_pre, preferred_element_type=jnp.float32) * grad_scale
    grad_neigh = jnp.dot(aggregate.T, grad_pre, preferred_element_type=jnp.float32) * grad_scale
    grad_bias = lax.optimization_barrier(jnp.sum(grad_pre.astype(jnp.float32), axis=0)) * grad_scale
    back_rows = jnp.dot(grad_pre, w_neigh.T, preferred_element_type=jnp.float32).astype(jnp.bfloat16)
    back_rows = back_rows.reshape(NBLOCKS, TILE, D)

    def backward_one(total, reader):
        source_ids = source_blocks(requests, tile_slot, reader)
        local_back = lax.dynamic_slice_in_dim(back_rows, reader * BLK_DEV, BLK_DEV, 0)
        selected = local_back[tile_dest[reader]].astype(jnp.float32)
        products = jnp.einsum('tij,tid->tjd', tile_vals[reader].astype(jnp.float32), selected)
        return (total.at[source_ids].add(products), None)
    total, _ = lax.scan(backward_one, jnp.zeros((NBLOCKS, TILE, D), jnp.float32), readers)
    self_term = jnp.dot(grad_pre, w_self.T, preferred_element_type=jnp.float32)
    feat_grad = (self_term + total.reshape(NODES, D)).astype(jnp.bfloat16).reshape(NBLOCKS, TILE, D)
    return (hidden.reshape(NBLOCKS, TILE, D), grad_self, grad_neigh, grad_bias, feat_grad)
```

```python
import functools
import math

import jax
import jax.numpy as jnp
from jax import lax
from jax.experimental import pallas as pl
from jax.experimental.pallas import tpu as pltpu
from jax.sharding import PartitionSpec as P

SPLIT = (4, 8, 2)
CHUNK = 4
LAG = 3

MESH = pl.DeviceIdType.MESH
F32 = jnp.float32
BF16 = jnp.bfloat16


def exchange_kernel(
    split,
    chunk,
    scale,
    req_ref,
    inv_ref,
    feats_ref,
    tiles_ref,
    ws_ref,
    wn_ref,
    bias_ref,
    ct_ref,
    hid_out,
    fg_out,
    grad_out,
    own,
    ct,
    tv,
    stage,
    src,
    tden,
    acc,
    gp,
    agg,
    back,
    hid,
    fg,
    cf,
    r1s,
    r1r,
    r2s,
    r2r,
    r3s,
    arr,
    g_all,
    g_core,
    g_xs,
    g_zs,
    g_piece,
    g_ys,
    g_fz,
    g_fx,
    g_fc,
    in_sem,
    out_sem,
    a_send,
    a_recv,
    b1_send,
    b1_recv,
    b2_send,
    b2_recv,
    r1_send,
    r1_recv,
    r2_send,
    r2_recv,
    r3_send,
    r3_recv,
    gc_send,
    gc_recv,
    gx_send,
    gx_recv,
    gz_send,
    gz_recv,
    gy_send,
    gy_recv,
    hz_send,
    hz_recv,
    hx_send,
    hx_recv,
    hc_send,
    hc_recv,
):
    nx, nz, nc = split
    slots = nx * nz * nc
    steps = slots // chunk
    y = lax.axis_index("rep")
    b = lax.axis_index("blk")
    x = lax.div(b, nz * nc)
    z = lax.rem(lax.div(b, nc), nz)
    c = lax.rem(b, nc)
    up = lax.rem(y + 1, 4)
    down = lax.rem(y + 3, 4)
    far = lax.rem(y + 2, 4)

    def shift(s):
        dc = lax.rem(s, nc)
        p = lax.div(s, nc)
        dx = lax.rem(p, nx)
        q = lax.div(p, nx)
        dz = lax.div(q + 1, 2) * (2 * lax.rem(q, 2) - 1)
        return dx, dz, dc

    def at(px, pz, pc):
        return (px * nz + pz) * nc + pc

    def reader(s):
        dx, dz, dc = shift(s)
        return at(lax.rem(x + dx, nx), lax.rem(z + dz + nz, nz), lax.rem(c + dc, nc))

    def owner(s):
        dx, dz, dc = shift(s)
        return at(
            lax.rem(x - dx + nx, nx), lax.rem(z - dz + nz, nz), lax.rem(c - dc + nc, nc)
        )

    def remote(source, target, send, recv, rep, blk):
        return pltpu.make_async_remote_copy(
            src_ref=source,
            dst_ref=target,
            send_sem=send,
            recv_sem=recv,
            device_id=(rep, blk),
            device_id_type=MESH,
        )

    load_own = pltpu.make_async_copy(feats_ref.at[:, y], own, in_sem.at[0])
    load_tiles = pltpu.make_async_copy(
        tiles_ref, tv.at[pl.ds(0, tiles_ref.shape[0])], in_sem.at[1]
    )
    load_ct = pltpu.make_async_copy(ct_ref, ct, in_sem.at[2])
    load_own.start()
    load_tiles.start()
    load_ct.start()

    barrier = pltpu.get_barrier_semaphore()

    def greet(s, carry):
        pl.semaphore_signal(barrier, inc=1, device_id=(y, reader(s)), device_id_type=MESH)
        return carry

    lax.fori_loop(1, slots, greet, 0)
    for d in range(1, 4):
        pl.semaphore_signal(
            barrier, inc=1, device_id=(lax.rem(y + d, 4), b), device_id_type=MESH
        )
    tv[tiles_ref.shape[0]] = jnp.zeros(tv.shape[1:], BF16)
    load_own.wait()

    def gather(s, carry):
        stage[s] = own[req_ref[reader(s)]]
        return carry

    lax.fori_loop(0, slots, gather, 0)
    src[0, y] = stage[0]
    acc[...] = jnp.zeros_like(acc)
    pl.semaphore_wait(barrier, slots - 1 + 3)

    def a_copy(s):
        return remote(
            stage.at[s], src.at[s, y], a_send.at[s], a_recv.at[s], y, reader(s)
        )

    def a_start(s, carry):
        a_copy(s).start()
        return carry

    lax.fori_loop(1, slots, a_start, 0)
    load_tiles.wait()

    def b1_copy(i, d):
        part = src.at[pl.ds(i * chunk, chunk), y]
        return remote(
            part, part, b1_send.at[i, d], b1_recv.at[i, d], (up, down)[d], b
        )

    def b1_wait(i, d):
        part = src.at[pl.ds(i * chunk, chunk), (down, up)[d]]
        remote(part, part, b1_send.at[i, d], b1_recv.at[i, d], (up, down)[d], b).wait_recv()

    def b2_copy(i, d):
        part = src.at[pl.ds(i * chunk, chunk), (down, up)[d], d]
        return remote(
            part, part, b2_send.at[i, d], b2_recv.at[i, d], (up, down)[d], b
        )

    def b2_wait(i, d):
        part = src.at[pl.ds(i * chunk, chunk), far, d]
        remote(part, part, b2_send.at[i, d], b2_recv.at[i, d], (up, down)[d], b).wait_recv()

    blocks = own.shape[0]
    rows = own.shape[1] * own.shape[2]
    width = 4 * rows
    feat = own.shape[-1]
    total = blocks * rows

    def forward(i, carry):
        @pl.when(i < steps)
        def _():
            @pl.when(i >= 0)
            def _():
                for k in range(chunk):
                    s = i * chunk + k
                    o = owner(s)
                    for d in range(blocks):
                        tden[i, pl.ds(d * rows, rows), pl.ds(k * width, width)] = tv[
                            inv_ref[d * slots + o]
                        ]

            for k in range(chunk):
                s = i * chunk + k

                @pl.when(s > 0)
                def _():
                    a_copy(s).wait_recv()

            for d in range(2):
                b1_copy(i, d).start()

        @pl.when(jnp.logical_and(i >= 1, i < steps + 1))
        def _():
            for d in range(2):
                b1_wait(i - 1, d)
            for d in range(2):
                b2_copy(i - 1, d).start()

        @pl.when(i >= 2)
        def _():
            for d in range(2):
                b2_wait(i - 2, d)
            blockset = src[pl.ds((i - 2) * chunk, chunk)].reshape(chunk * width, feat)
            acc[...] += jnp.dot(tden[i - 2], blockset, preferred_element_type=F32)

        return carry

    lax.fori_loop(0, steps + 2, forward, 0)

    load_ct.wait()
    part = total // 4
    per = blocks // 4

    def dense(n, carry):
        here = pl.ds(n * part, part)
        blk = pl.ds(n * per, per)
        mine = own[blk].reshape(part, feat)
        mixed = acc[here, :].astype(BF16)
        agg[here, :] = mixed
        pre = jnp.dot(mine, ws_ref[...], preferred_element_type=F32)
        pre = pre + jnp.dot(mixed, wn_ref[...], preferred_element_type=F32) + bias_ref[...]
        gate = 1.0 / (1.0 + jnp.exp(-pre))
        hid[blk] = (pre * gate).astype(BF16).reshape(per, rows, feat)
        down_grad = ct[blk].reshape(part, feat).astype(F32)
        grad = (down_grad * gate * (1.0 + pre * (1.0 - gate))).astype(BF16)
        gp[here, :] = grad
        back[here, :] = lax.dot_general(
            grad, wn_ref[...], (((1,), (1,)), ((), ())), preferred_element_type=F32
        ).astype(BF16)
        return carry

    lax.fori_loop(0, 4, dense, 0)
    save_hid = pltpu.make_async_copy(hid, hid_out, out_sem.at[0])
    save_hid.start()

    def r1_copy(j, d):
        here = pl.ds(j * chunk, chunk)
        return remote(
            r1s.at[here, d],
            r1r.at[here, d],
            r1_send.at[j, d],
            r1_recv.at[j, d],
            (up, down)[d],
            b,
        )

    def r2_copy(j, d):
        here = pl.ds(j * chunk, chunk)
        return remote(
            r2s.at[here, d],
            r2r.at[here, d],
            r2_send.at[j, d],
            r2_recv.at[j, d],
            (up, down)[d],
            b,
        )

    def r3_copy(s):
        return remote(r3s.at[s], arr.at[s], r3_send.at[s], r3_recv.at[s], y, owner(s))

    half = nx * nz
    other = at(x, z, nc - 1 - c) if nc == 2 else b

    def core_copy():
        return remote(
            g_all.at[pl.ds((1 - c) * half, half)], g_core, gc_send, gc_recv, y, other
        )

    def x_copy(d):
        peer = lax.rem(x + d, nx)
        return remote(
            g_all.at[pl.ds(c * half + peer * nz, nz)],
            g_xs.at[d],
            gx_send.at[d],
            gx_recv.at[d],
            y,
            at(peer, z, c),
        )

    def z_copy(d):
        peer = lax.rem(z + d, nz)
        return remote(
            g_all.at[c * half + x * nz + peer],
            g_zs.at[d],
            gz_send.at[d],
            gz_recv.at[d],
            y,
            at(x, peer, c),
        )

    def y_copy(d):
        return remote(
            g_piece, g_ys.at[y], gy_send.at[d], gy_recv.at[d], lax.rem(y + d, 4), b
        )

    def zz_copy(d):
        return remote(
            g_fz.at[z],
            g_fz.at[z],
            hz_send.at[d],
            hz_recv.at[d],
            y,
            at(x, lax.rem(z + d, nz), c),
        )

    def xx_copy(d):
        return remote(
            g_fz, g_fx.at[x], hx_send.at[d], hx_recv.at[d], y, at(lax.rem(x + d, nx), z, c)
        )

    def cc_copy():
        return remote(g_fx, g_fc.at[c], hc_send, hc_recv, y, other)

    def grads():
        feat_rows = own[...].reshape(total, feat)
        grad = gp[...]
        first = lax.dot_general(
            feat_rows, grad, (((0,), (0,)), ((), ())), preferred_element_type=F32
        )
        second = lax.dot_general(
            agg[...], grad, (((0,), (0,)), ((), ())), preferred_element_type=F32
        )
        pieces = nc * half
        tall = 2 * feat // pieces
        g_all[...] = jnp.zeros_like(g_all)
        g_all[pl.ds(0, pieces // 2), pl.ds(0, tall), :] = (first * scale).reshape(
            pieces // 2, tall, feat
        )
        g_all[pl.ds(pieces // 2, pieces // 2), pl.ds(0, tall), :] = (second * scale).reshape(
            pieces // 2, tall, feat
        )
        g_all[0, pl.ds(tall, 1), :] = (
            jnp.sum(grad.astype(F32), axis=0, keepdims=True) * scale
        )
        if nc == 2:
            core_copy().start()

    def grads_core():
        if nc == 2:
            core_copy().wait_recv()
            here = pl.ds(c * half, half)
            g_all[here] = g_all[here] + g_core[...]
        for d in range(1, nx):
            x_copy(d).start()

    def grads_x():
        here = pl.ds(c * half + x * nz, nz)
        value = g_all[here]
        for d in range(1, nx):
            x_copy(d).wait_recv()
            value = value + g_xs[d]
        g_all[here] = value
        for d in range(1, nz):
            z_copy(d).start()

    def grads_z():
        value = g_all[c * half + x * nz + z]
        for d in range(1, nz):
            z_copy(d).wait_recv()
            value = value + g_zs[d]
        g_piece[...] = value
        g_ys[y] = value
        for d in range(1, 4):
            y_copy(d).start()

    def grads_y():
        for d in range(1, 4):
            source = lax.rem(y + 4 - d, 4)
            remote(
                g_piece, g_ys.at[source], gy_send.at[d], gy_recv.at[d], y, b
            ).wait_recv()
        g_fz[z] = (g_ys[0] + g_ys[1]) + (g_ys[2] + g_ys[3])
        for d in range(1, nz):
            zz_copy(d).start()

    def grads_zz():
        for d in range(1, nz):
            source = lax.rem(z + nz - d, nz)
            remote(
                g_fz.at[z], g_fz.at[source], hz_send.at[d], hz_recv.at[d], y, b
            ).wait_recv()
        g_fx[x] = g_fz[...]
        for d in range(1, nx):
            xx_copy(d).start()

    def grads_xx():
        for d in range(1, nx):
            source = lax.rem(x + nx - d, nx)
            remote(
                g_fz, g_fx.at[source], hx_send.at[d], hx_recv.at[d], y, b
            ).wait_recv()
        g_fc[c] = g_fx[...]
        if nc == 2:
            cc_copy().start()

    def grads_cc():
        if nc == 2:
            remote(g_fx, g_fc.at[1 - c], hc_send, hc_recv, y, b).wait_recv()

    def collect(j):
        lane = lax.broadcasted_iota(jnp.int32, (1, chunk * rows), 1)
        target = lax.rem(lane, rows)
        for k in range(chunk):
            s = j * chunk + k
            inside = jnp.logical_and(lane >= k * rows, lane < (k + 1) * rows)
            target = target + jnp.where(inside, req_ref[reader(s)] * rows, 0)

            @pl.when(s > 0)
            def _():
                r3_copy(s).wait_recv()

        row = lax.broadcasted_iota(jnp.int32, (total, chunk * rows), 0)
        pick = jnp.where(row == target, 1.0, 0.0).astype(BF16)
        came = arr[pl.ds(j * chunk, chunk)].reshape(chunk * rows, feat)
        acc[...] += jnp.dot(pick, came, preferred_element_type=F32)

    stages = (grads_core, grads_x, grads_z, grads_y, grads_zz, grads_xx)

    def backward(i, carry):
        j = steps - 1 - i

        @pl.when(i < steps)
        def _():
            product = lax.dot_general(
                tden[j], back[...], (((0,), (0,)), ((), ())), preferred_element_type=F32
            )
            here = pl.ds(j * chunk, chunk)
            cf[...] = product.reshape(chunk, 4, 2, rows // 2, feat)
            r1s[here] = cf[:, far].astype(BF16)
            r2s[here, 0] = cf[:, up].astype(BF16)
            r2s[here, 1] = cf[:, down].astype(BF16)
            r3s[here] = cf[:, y].astype(BF16)
            for d in range(2):
                r1_copy(j, d).start()

        @pl.when(jnp.logical_and(i >= 1, i < steps + 1))
        def _():
            n = j + 1
            here = pl.ds(n * chunk, chunk)
            for d in range(2):
                r1_copy(n, d).wait_recv()
                r2s[here, d, d] = (
                    r2s[here, d, d].astype(F32) + r1r[here, d].astype(F32)
                ).astype(BF16)
            for d in range(2):
                r2_copy(n, d).start()

        @pl.when(jnp.logical_and(i >= 2, i < steps + 2))
        def _():
            n = j + 2
            here = pl.ds(n * chunk, chunk)
            for d in range(2):
                r2_copy(n, d).wait_recv()
            r3s[here] = (
                r3s[here].astype(F32) + r2r[here, 0].astype(F32) + r2r[here, 1].astype(F32)
            ).astype(BF16)
            for k in range(chunk):
                s = n * chunk + k

                @pl.when(s > 0)
                def _():
                    r3_copy(s).start()

        @pl.when(i == 0)
        def _():
            grads()
            grad = gp[...]
            acc[...] = lax.dot_general(
                grad, ws_ref[...], (((1,), (1,)), ((), ())), preferred_element_type=F32
            )

        for n, stage_fn in enumerate(stages):

            @pl.when(i == min(2 + 2 * n, steps + 1))
            def _(stage_fn=stage_fn):
                stage_fn()

        @pl.when(i >= 2 + LAG)
        def _():
            collect(j + 2 + LAG)

        return carry

    lax.fori_loop(0, steps + 2, backward, 0)
    arr[0] = r3s[0]
    for n in range(LAG):
        if LAG - 1 - n < steps:
            collect(jnp.int32(LAG - 1 - n))
    fg[...] = acc[...].astype(BF16).reshape(fg.shape)
    save_fg = pltpu.make_async_copy(fg, fg_out, out_sem.at[1])
    save_fg.start()
    grads_cc()
    save_grad = pltpu.make_async_copy(g_fc, grad_out, out_sem.at[2])
    save_grad.start()

    def sent(s, carry):
        a_copy(s).wait_send()
        r3_copy(s).wait_send()
        return carry

    lax.fori_loop(1, slots, sent, 0)

    def sent_y(i, carry):
        for d in range(2):
            b1_copy(i, d).wait_send()
            b2_copy(i, d).wait_send()
            r1_copy(i, d).wait_send()
            r2_copy(i, d).wait_send()
        return carry

    lax.fori_loop(0, steps, sent_y, 0)
    if nc == 2:
        core_copy().wait_send()
        cc_copy().wait_send()
    for d in range(1, nx):
        x_copy(d).wait_send()
        xx_copy(d).wait_send()
    for d in range(1, nz):
        z_copy(d).wait_send()
        zz_copy(d).wait_send()
    for d in range(1, 4):
        y_copy(d).wait_send()
    save_hid.wait()
    save_fg.wait()
    save_grad.wait()


def finish_kernel(pieces, tall, grad_ref, hid_ref, fg_ref, hid_o, gs_o, gn_o, gb_o, fg_o):
    feat = grad_ref.shape[-1]
    value = grad_ref[...]
    gs_o[...] = value[: pieces // 2, :tall, :].reshape(feat, feat)
    gn_o[...] = value[pieces // 2 :, :tall, :].reshape(feat, feat)
    gb_o[...] = value[0, tall : tall + 1, :]
    hid_o[...] = hid_ref[...]
    fg_o[...] = fg_ref[...]


def on_device(feats, requests, tile_dest, tile_slot, tile_vals, w_self, w_neigh, bias, cotangent):
    owners = lax.axis_size("blk")
    replicas = lax.axis_size("rep")
    nx, nz, nc = SPLIT
    chunk = CHUNK
    steps = owners // chunk
    blocks, tile_rows, feat = feats.shape
    rows = tile_rows // replicas
    total = blocks * rows
    tiles = tile_vals.shape[1]
    pieces = nc * nx * nz
    tall = 2 * feat // pieces
    scale = 1.0 / math.sqrt(owners * blocks * tile_rows)

    number = jnp.arange(tiles, dtype=jnp.int32)
    hit = jnp.logical_and(
        tile_dest[0][None, None, :] == jnp.arange(blocks, dtype=jnp.int32)[:, None, None],
        tile_slot[0][None, None, :] == jnp.arange(owners, dtype=jnp.int32)[None, :, None],
    )
    inverse = tiles + jnp.sum(jnp.where(hit, number - tiles, 0), axis=-1)
    inverse = inverse.reshape(blocks * owners)

    vmem = pltpu.VMEM
    sem = pltpu.SemaphoreType.DMA
    piece = (tall + 1, feat)
    scratch = [
        vmem((blocks, 2, rows // 2, feat), BF16),
        vmem((blocks, rows, feat), BF16),
        vmem((tiles + 1, rows, tile_rows), BF16),
        vmem((owners, 2, rows // 2, feat), BF16),
        vmem((owners, 4, 2, rows // 2, feat), BF16),
        vmem((steps, total, chunk * tile_rows), BF16),
        vmem((total, feat), F32),
        vmem((total, feat), BF16),
        vmem((total, feat), BF16),
        vmem((total, feat), BF16),
        vmem((blocks, rows, feat), BF16),
        vmem((blocks, rows, feat), BF16),
        vmem((chunk, 4, 2, rows // 2, feat), F32),
        vmem((owners, 2, rows // 2, feat), BF16),
        vmem((owners, 2, rows // 2, feat), BF16),
        vmem((owners, 2, 2, rows // 2, feat), BF16),
        vmem((owners, 2, 2, rows // 2, feat), BF16),
        vmem((owners, 2, rows // 2, feat), BF16),
        vmem((owners, 2, rows // 2, feat), BF16),
        vmem((pieces, *piece), F32),
        vmem((nx * nz, *piece), F32),
        vmem((nx, nz, *piece), F32),
        vmem((nz, *piece), F32),
        vmem(piece, F32),
        vmem((4, *piece), F32),
        vmem((nz, *piece), F32),
        vmem((nx, nz, *piece), F32),
        vmem((nc, nx, nz, *piece), F32),
        sem((3,)),
        sem((3,)),
        sem((owners,)),
        sem((owners,)),
        sem((steps, 2)),
        sem((steps, 2)),
        sem((steps, 2)),
        sem((steps, 2)),
        sem((steps, 2)),
        sem((steps, 2)),
        sem((steps, 2)),
        sem((steps, 2)),
        sem((owners,)),
        sem((owners,)),
        sem,
        sem,
        sem((nx,)),
        sem((nx,)),
        sem((nz,)),
        sem((nz,)),
        sem((4,)),
        sem((4,)),
        sem((nz,)),
        sem((nz,)),
        sem((nx,)),
        sem((nx,)),
        sem,
        sem,
    ]
    smem = pl.BlockSpec(memory_space=pltpu.SMEM)
    hbm = pl.BlockSpec(memory_space=pl.ANY)
    whole = pl.BlockSpec(memory_space=pltpu.VMEM)
    hid, fg, grad = pl.pallas_call(
        functools.partial(exchange_kernel, SPLIT, chunk, scale),
        out_shape=(
            jax.ShapeDtypeStruct((blocks, rows, feat), BF16),
            jax.ShapeDtypeStruct((blocks, rows, feat), BF16),
            jax.ShapeDtypeStruct((nc, nx, nz, *piece), F32),
        ),
        in_specs=[smem, smem, hbm, hbm, whole, whole, whole, hbm],
        out_specs=(hbm, hbm, hbm),
        scratch_shapes=scratch,
        compiler_params=pltpu.CompilerParams(
            collective_id=0, has_side_effects=True, vmem_limit_bytes=60 << 20
        ),
    )(
        requests[0],
        inverse,
        feats.reshape(blocks, replicas, 2, rows // 2, feat),
        tile_vals[0],
        w_self,
        w_neigh,
        bias.reshape(1, feat),
        cotangent,
    )
    hidden, grad_self, grad_neigh, grad_bias, feat_grad = pl.pallas_call(
        functools.partial(finish_kernel, pieces, tall),
        out_shape=(
            jax.ShapeDtypeStruct((blocks, rows, feat), BF16),
            jax.ShapeDtypeStruct((feat, feat), F32),
            jax.ShapeDtypeStruct((feat, feat), F32),
            jax.ShapeDtypeStruct((1, feat), F32),
            jax.ShapeDtypeStruct((blocks, rows, feat), BF16),
        ),
        in_specs=[whole, whole, whole],
        out_specs=(whole, whole, whole, whole, whole),
    )(grad.reshape(pieces, *piece), hid, fg)
    return (hidden, grad_self, grad_neigh, grad_bias.reshape(feat), feat_grad)


def solution(mesh):
    in_specs = (
        P("blk", None, None),
        P("blk", None),
        P("blk", None),
        P("blk", None),
        P("blk", None, "rep", None),
        P(),
        P(),
        P(),
        P("blk", "rep", None),
    )
    out_specs = (P("blk", "rep", None), P(), P(), P(), P("blk", "rep", None))
    return jax.shard_map(
        on_device, mesh=mesh, in_specs=in_specs, out_specs=out_specs, check_vma=False
    )
```

```python
import functools
import math

import jax
import jax.numpy as jnp
from jax import lax
from jax.experimental import pallas as pl
from jax.experimental.pallas import tpu as pltpu
from jax.sharding import PartitionSpec as P

SPLIT = (4, 8, 2)
CHUNK = 4
LAG = 5
HOP1, HOP2 = 2, 4

GRADS_AT, GRADS_GAP = 3, 2

MESH = pl.DeviceIdType.MESH
F32 = jnp.float32
BF16 = jnp.bfloat16


def exchange_kernel(
    split,
    chunk,
    scale,
    req_ref,
    inv_ref,
    feats_ref,
    tiles_ref,
    ws_ref,
    wn_ref,
    bias_ref,
    ct_ref,
    hid_out,
    fg_out,
    grad_out,
    fv,
    ct,
    tv,
    stage,
    stage_near,
    src,
    tden,
    acc,
    gp,
    agg,
    back,
    hid,
    fg,
    cf,
    r1s,
    r1r,
    r2s,
    r2r,
    r3s,
    arr,
    g_all,
    g_core,
    g_xs,
    g_zs,
    g_piece,
    g_ys,
    g_fz,
    g_fx,
    g_fc,
    in_sem,
    out_sem,
    a_send,
    a_recv,
    near_send,
    near_recv,
    b1_send,
    b1_recv,
    b2_send,
    b2_recv,
    r1_send,
    r1_recv,
    r2_send,
    r2_recv,
    r3_send,
    r3_recv,
    gc_send,
    gc_recv,
    gx_send,
    gx_recv,
    gz_send,
    gz_recv,
    gy_send,
    gy_recv,
    hz_send,
    hz_recv,
    hx_send,
    hx_recv,
    hc_send,
    hc_recv,
):
    nx, nz, nc = split
    slots = nx * nz * nc
    steps = slots // chunk
    near = nx * nc
    skip = near // chunk
    y = lax.axis_index("rep")
    b = lax.axis_index("blk")
    x = lax.div(b, nz * nc)
    z = lax.rem(lax.div(b, nc), nz)
    c = lax.rem(b, nc)
    up = lax.rem(y + 1, 4)
    down = lax.rem(y + 3, 4)
    far = lax.rem(y + 2, 4)

    def shift(s):
        dc = lax.rem(s, nc)
        p = lax.div(s, nc)
        dx = lax.rem(p, nx)
        q = lax.div(p, nx)
        dz = lax.div(q + 1, 2) * (2 * lax.rem(q, 2) - 1)
        return dx, dz, dc

    def at(px, pz, pc):
        return (px * nz + pz) * nc + pc

    def reader(s):
        dx, dz, dc = shift(s)
        return at(lax.rem(x + dx, nx), lax.rem(z + dz + nz, nz), lax.rem(c + dc, nc))

    def owner(s):
        dx, dz, dc = shift(s)
        return at(
            lax.rem(x - dx + nx, nx), lax.rem(z - dz + nz, nz), lax.rem(c - dc + nc, nc)
        )

    def remote(source, target, send, recv, rep, blk):
        return pltpu.make_async_remote_copy(
            src_ref=source,
            dst_ref=target,
            send_sem=send,
            recv_sem=recv,
            device_id=(rep, blk),
            device_id_type=MESH,
        )

    load_own = pltpu.make_async_copy(feats_ref, fv, in_sem.at[0])
    load_tiles = pltpu.make_async_copy(
        tiles_ref, tv.at[pl.ds(0, tiles_ref.shape[0])], in_sem.at[1]
    )
    load_ct = pltpu.make_async_copy(ct_ref, ct, in_sem.at[2])
    load_own.start()
    load_tiles.start()
    load_ct.start()

    barrier = pltpu.get_barrier_semaphore()

    def greet(s, carry):
        pl.semaphore_signal(barrier, inc=1, device_id=(y, reader(s)), device_id_type=MESH)
        return carry

    lax.fori_loop(1, slots, greet, 0)
    for d in range(1, 4):
        pl.semaphore_signal(
            barrier, inc=1, device_id=(lax.rem(y + d, 4), b), device_id_type=MESH
        )
    tv[tiles_ref.shape[0]] = jnp.zeros(tv.shape[1:], BF16)
    load_own.wait()

    def gather(s, carry):
        stage[s] = fv[req_ref[reader(s)], y]
        return carry

    lax.fori_loop(near, slots, gather, 0)

    def gather_near(s, carry):
        stage_near[s] = fv[req_ref[reader(s)]]
        return carry

    lax.fori_loop(1, near, gather_near, 0)
    src[0] = fv[req_ref[b]]
    acc[...] = jnp.zeros_like(acc)
    blocks = fv.shape[0]
    rows = fv.shape[2] * fv.shape[3]
    width = 4 * rows
    feat = fv.shape[-1]
    total = blocks * rows
    load_tiles.wait()

    def spread(i, carry):
        for k in range(chunk):
            o = owner(i * chunk + k)
            for d in range(blocks):
                tden[i, pl.ds(d * rows, rows), pl.ds(k * width, width)] = tv[
                    inv_ref[d * slots + o]
                ]
        return carry

    lax.fori_loop(0, steps, spread, 0)
    pl.semaphore_wait(barrier, slots - 1 + 3)

    def a_copy(s):
        return remote(
            stage.at[s], src.at[s, y], a_send, a_recv.at[lax.div(s, chunk)], y, reader(s)
        )

    def a_start(s, carry):
        a_copy(s).start()
        return carry

    lax.fori_loop(near, slots, a_start, 0)

    def near_start(s, carry):
        remote(stage_near.at[s], src.at[s], near_send, near_recv, y, reader(s)).start()
        return carry

    lax.fori_loop(1, near, near_start, 0)

    def wait_recv(target, recv):
        remote(target, target, in_sem.at[0], recv, up, b).wait_recv()

    def wait_send(source, send):
        remote(source, source, send, in_sem.at[0], up, b).wait_send()

    def b1_copy(i, d):
        part = src.at[pl.ds(i * chunk, chunk), y]
        return remote(part, part, b1_send, b1_recv.at[i], (up, down)[d], b)

    def b2_copy(i, d):
        part = src.at[pl.ds(i * chunk, chunk), (down, up)[d], d]
        return remote(part, part, b2_send, b2_recv.at[i], (up, down)[d], b)

    def mix(i):
        blockset = src[pl.ds(i * chunk, chunk)].reshape(chunk * width, feat)
        acc[...] += jnp.dot(tden[i], blockset, preferred_element_type=F32)

    def forward(i, carry):
        @pl.when(i < steps)
        def _():
            wait_recv(src.at[pl.ds(i * chunk, chunk), y], a_recv.at[i])
            for d in range(2):
                b1_copy(i, d).start()

        @pl.when(jnp.logical_and(i >= skip + HOP1, i < steps + HOP1))
        def _():
            wait_recv(src.at[pl.ds((i - HOP1) * chunk, chunk), pl.ds(0, 2)], b1_recv.at[i - HOP1])
            for d in range(2):
                b2_copy(i - HOP1, d).start()

        @pl.when(i >= skip + HOP2)
        def _():
            wait_recv(src.at[pl.ds((i - HOP2) * chunk, chunk), far], b2_recv.at[i - HOP2])
            mix(i - HOP2)

        @pl.when(i == steps // 2)
        def _():
            wait_recv(src.at[pl.ds(1, near - 1)], near_recv)
            for n in range(skip):
                mix(n)

        return carry

    lax.fori_loop(skip, steps + HOP2, forward, 0)

    load_ct.wait()
    part = total // 4
    per = blocks // 4

    def dense(n, carry):
        here = pl.ds(n * part, part)
        blk = pl.ds(n * per, per)
        mine = fv[blk, y].reshape(part, feat)
        mixed = acc[here, :].astype(BF16)
        agg[here, :] = mixed
        pre = jnp.dot(mine, ws_ref[...], preferred_element_type=F32)
        pre = pre + jnp.dot(mixed, wn_ref[...], preferred_element_type=F32) + bias_ref[...]
        gate = 1.0 / (1.0 + jnp.exp(-pre))
        hid[blk] = (pre * gate).astype(BF16).reshape(per, rows, feat)
        down_grad = ct[blk].reshape(part, feat).astype(F32)
        grad = (down_grad * gate * (1.0 + pre * (1.0 - gate))).astype(BF16)
        gp[here, :] = grad
        back[here, :] = lax.dot_general(
            grad, wn_ref[...], (((1,), (1,)), ((), ())), preferred_element_type=F32
        ).astype(BF16)
        return carry

    lax.fori_loop(0, 4, dense, 0)
    save_hid = pltpu.make_async_copy(hid, hid_out, out_sem.at[0])
    save_hid.start()

    def r1_copy(j, d):
        here = pl.ds(j * chunk, chunk)
        return remote(
            r1s.at[here, d],
            r1r.at[here, d],
            r1_send,
            r1_recv.at[j],
            (up, down)[d],
            b,
        )

    def r2_copy(j, d):
        here = pl.ds(j * chunk, chunk)
        return remote(
            r2s.at[here, d],
            r2r.at[here, d],
            r2_send,
            r2_recv.at[j],
            (up, down)[d],
            b,
        )

    def r3_copy(s):
        return remote(
            r3s.at[s], arr.at[s], r3_send, r3_recv.at[lax.div(s, chunk)], y, owner(s)
        )

    half = nx * nz
    other = at(x, z, nc - 1 - c) if nc == 2 else b

    def core_copy():
        return remote(
            g_all.at[pl.ds((1 - c) * half, half)], g_core, gc_send, gc_recv, y, other
        )

    def x_copy(d):
        peer = lax.rem(x + d, nx)
        return remote(
            g_all.at[pl.ds(c * half + peer * nz, nz)],
            g_xs.at[d],
            gx_send,
            gx_recv,
            y,
            at(peer, z, c),
        )

    def z_copy(d):
        peer = lax.rem(z + d, nz)
        return remote(
            g_all.at[c * half + x * nz + peer],
            g_zs.at[d],
            gz_send,
            gz_recv,
            y,
            at(x, peer, c),
        )

    def y_copy(d):
        return remote(
            g_piece, g_ys.at[y], gy_send, gy_recv.at[d], lax.rem(y + d, 4), b
        )

    def zz_copy(d):
        return remote(
            g_fz.at[z],
            g_fz.at[z],
            hz_send,
            hz_recv.at[d],
            y,
            at(x, lax.rem(z + d, nz), c),
        )

    def xx_copy(d):
        return remote(
            g_fz, g_fx.at[x], hx_send, hx_recv.at[d], y, at(lax.rem(x + d, nx), z, c)
        )

    def cc_copy():
        return remote(g_fx, g_fc.at[c], hc_send, hc_recv, y, other)

    def grads():
        feat_rows = fv[:, y].reshape(total, feat)
        grad = gp[...]
        first = lax.dot_general(
            feat_rows, grad, (((0,), (0,)), ((), ())), preferred_element_type=F32
        )
        second = lax.dot_general(
            agg[...], grad, (((0,), (0,)), ((), ())), preferred_element_type=F32
        )
        pieces = nc * half
        tall = 2 * feat // pieces
        g_all[:, :, pl.ds(feat, 128)] = jnp.zeros((pieces, tall, 128), F32)
        g_all[pl.ds(0, pieces // 2), :, pl.ds(0, feat)] = (first * scale).reshape(
            pieces // 2, tall, feat
        )
        g_all[pl.ds(pieces // 2, pieces // 2), :, pl.ds(0, feat)] = (second * scale).reshape(
            pieces // 2, tall, feat
        )
        down_sum = jnp.sum(grad.astype(F32), axis=0, keepdims=True) * scale
        for n in range(feat // 128):
            g_all[0, pl.ds(n, 1), pl.ds(feat, 128)] = down_sum[:, n * 128 : (n + 1) * 128]
        if nc == 2:
            core_copy().start()

    def grads_core():
        if nc == 2:
            core_copy().wait_recv()
            here = pl.ds(c * half, half)
            g_all[here] = g_all[here] + g_core[...]
        for d in range(1, nx):
            x_copy(d).start()

    def grads_x():
        here = pl.ds(c * half + x * nz, nz)
        value = g_all[here]
        wait_recv(g_xs.at[pl.ds(1, nx - 1)], gx_recv)
        for d in range(1, nx):
            value = value + g_xs[d]
        g_all[here] = value
        for d in range(1, nz):
            z_copy(d).start()

    def grads_z():
        value = g_all[c * half + x * nz + z]
        wait_recv(g_zs.at[pl.ds(1, nz - 1)], gz_recv)
        for d in range(1, nz):
            value = value + g_zs[d]
        g_piece[...] = value
        g_ys[y] = value
        for d in range(1, 4):
            y_copy(d).start()

    def grads_y():
        for d in range(1, 4):
            source = lax.rem(y + 4 - d, 4)
            wait_recv(g_ys.at[source], gy_recv.at[d])
        g_fz[z] = (g_ys[0] + g_ys[1]) + (g_ys[2] + g_ys[3])
        for d in range(1, nz):
            zz_copy(d).start()

    def grads_zz():
        for d in range(1, nz):
            source = lax.rem(z + nz - d, nz)
            wait_recv(g_fz.at[source], hz_recv.at[d])
        g_fx[x] = g_fz[...]
        for d in range(1, nx):
            xx_copy(d).start()

    def grads_xx():
        for d in range(1, nx):
            source = lax.rem(x + nx - d, nx)
            wait_recv(g_fx.at[source], hx_recv.at[d])
        g_fc[c] = g_fx[...]
        if nc == 2:
            cc_copy().start()

    def grads_cc():
        if nc == 2:
            wait_recv(g_fc.at[1 - c], hc_recv)

    def collect(j):
        lane = lax.broadcasted_iota(jnp.int32, (1, chunk * rows), 1)
        target = lax.rem(lane, rows)
        for k in range(chunk):
            s = j * chunk + k
            inside = jnp.logical_and(lane >= k * rows, lane < (k + 1) * rows)
            target = target + jnp.where(inside, req_ref[reader(s)] * rows, 0)

        @pl.when(j > 0)
        def _():
            wait_recv(arr.at[pl.ds(j * chunk, chunk)], r3_recv.at[j])

        @pl.when(j == 0)
        def _():
            wait_recv(arr.at[pl.ds(1, chunk - 1)], r3_recv.at[0])

        row = lax.broadcasted_iota(jnp.int32, (total, chunk * rows), 0)
        pick = jnp.where(row == target, 1.0, 0.0).astype(BF16)
        came = arr[pl.ds(j * chunk, chunk)].reshape(chunk * rows, feat)
        acc[...] += jnp.dot(pick, came, preferred_element_type=F32)

    stages = (grads_core, grads_x, grads_z, grads_y, grads_zz, grads_xx)

    def turn(i):
        n = lax.div(i, skip)
        odd = lax.rem(n, 2)
        early = nz - 1 - lax.div(n, 2)
        late = lax.rem(lax.div(n + 1, 2), nz // 2)
        return ((1 - odd) * early + odd * late) * skip + lax.rem(i, skip)

    def backward(i, carry):

        @pl.when(i < steps)
        def _():
            j = turn(i)
            product = lax.dot_general(
                tden[j], back[...], (((0,), (0,)), ((), ())), preferred_element_type=F32
            )
            here = pl.ds(j * chunk, chunk)
            cf[...] = product.reshape(chunk, 4, 2, rows // 2, feat)
            r1s[here] = cf[:, far].astype(BF16)
            r2s[here, 0] = cf[:, up].astype(BF16)
            r2s[here, 1] = cf[:, down].astype(BF16)
            r3s[here] = cf[:, y].astype(BF16)
            for d in range(2):
                r1_copy(j, d).start()

        @pl.when(jnp.logical_and(i >= HOP1, i < steps + HOP1))
        def _():
            n = turn(i - HOP1)
            here = pl.ds(n * chunk, chunk)
            wait_recv(r1r.at[here], r1_recv.at[n])
            for d in range(2):
                r2s[here, d, d] = (
                    r2s[here, d, d].astype(F32) + r1r[here, d].astype(F32)
                ).astype(BF16)
            for d in range(2):
                r2_copy(n, d).start()

        @pl.when(jnp.logical_and(i >= HOP2, i < steps + HOP2))
        def _():
            n = turn(i - HOP2)
            here = pl.ds(n * chunk, chunk)
            wait_recv(r2r.at[here], r2_recv.at[n])
            r3s[here] = (
                r3s[here].astype(F32) + r2r[here, 0].astype(F32) + r2r[here, 1].astype(F32)
            ).astype(BF16)
            for k in range(chunk):
                s = n * chunk + k

                @pl.when(s > 0)
                def _():
                    r3_copy(s).start()

                @pl.when(s == 0)
                def _():
                    arr[0] = r3s[0]

        @pl.when(i == GRADS_AT)
        def _():
            grads()

        @pl.when(i == GRADS_AT - 1)
        def _():
            grad = gp[...]
            acc[...] = lax.dot_general(
                grad, ws_ref[...], (((1,), (1,)), ((), ())), preferred_element_type=F32
            )

        for n, stage_fn in enumerate(stages):

            @pl.when(i == min(GRADS_AT + GRADS_GAP * (n + 1), steps + HOP2 - 1))
            def _(stage_fn=stage_fn):
                stage_fn()

        @pl.when(i >= HOP2 + LAG)
        def _():
            collect(turn(i - HOP2 - LAG))

        return carry

    lax.fori_loop(0, steps + HOP2, backward, 0)
    for n in range(LAG):
        collect(turn(jnp.int32(steps - LAG + n)))
    fg[...] = acc[...].astype(BF16).reshape(fg.shape)
    save_fg = pltpu.make_async_copy(fg, fg_out, out_sem.at[1])
    save_fg.start()
    grads_cc()
    save_grad = pltpu.make_async_copy(g_fc, grad_out, out_sem.at[2])
    save_grad.start()

    wait_send(stage.at[pl.ds(near, slots - near)], a_send)
    wait_send(stage_near.at[pl.ds(1, near - 1)], near_send)
    wait_send(src.at[pl.ds(near, slots - near), pl.ds(0, 2)], b1_send)
    wait_send(src.at[pl.ds(near, slots - near), 0], b2_send)
    wait_send(r1s, r1_send)
    wait_send(r2s, r2_send)
    wait_send(r3s.at[pl.ds(1, slots - 1)], r3_send)
    if nc == 2:
        core_copy().wait_send()
        cc_copy().wait_send()
    wait_send(g_xs.at[pl.ds(1, nx - 1)], gx_send)
    wait_send(g_zs.at[pl.ds(1, nz - 1)], gz_send)
    wait_send(g_ys.at[pl.ds(0, 3)], gy_send)
    wait_send(g_fz.at[pl.ds(0, nz - 1)], hz_send)
    wait_send(g_fx.at[pl.ds(0, nx - 1)], hx_send)
    save_hid.wait()
    save_fg.wait()
    save_grad.wait()


def finish_kernel(grad_ref, hid_ref, fg_ref, hid_o, gs_o, gn_o, gb_o, fg_o):
    pieces = grad_ref.shape[0]
    feat = gs_o.shape[0]
    gs_o[...] = grad_ref[pl.ds(0, pieces // 2), :, pl.ds(0, feat)].reshape(feat, feat)
    gn_o[...] = grad_ref[pl.ds(pieces // 2, pieces // 2), :, pl.ds(0, feat)].reshape(feat, feat)
    for n in range(feat // 128):
        gb_o[:, pl.ds(n * 128, 128)] = grad_ref[0, pl.ds(n, 1), pl.ds(feat, 128)]
    hid_o[...] = hid_ref[...]
    fg_o[...] = fg_ref[...]


def on_device(feats, requests, tile_dest, tile_slot, tile_vals, w_self, w_neigh, bias, cotangent):
    owners = lax.axis_size("blk")
    replicas = lax.axis_size("rep")
    nx, nz, nc = SPLIT
    chunk = CHUNK
    steps = owners // chunk
    blocks, tile_rows, feat = feats.shape
    rows = tile_rows // replicas
    total = blocks * rows
    tiles = tile_vals.shape[1]
    pieces = nc * nx * nz
    tall = 2 * feat // pieces
    scale = 1.0 / math.sqrt(owners * blocks * tile_rows)

    number = jnp.arange(tiles, dtype=jnp.int32)
    code = tile_dest[0] * owners + tile_slot[0]
    place = jnp.arange(blocks * owners, dtype=jnp.int32)
    inverse = tiles + jnp.sum(
        jnp.where(code[None, :] == place[:, None], number[None, :] - tiles, 0), axis=-1
    )

    vmem = pltpu.VMEM
    sem = pltpu.SemaphoreType.DMA
    piece = (tall, feat + 128)
    scratch = [
        vmem((blocks, 4, 2, rows // 2, feat), BF16),
        vmem((blocks, rows, feat), BF16),
        vmem((tiles + 1, rows, tile_rows), BF16),
        vmem((owners, 2, rows // 2, feat), BF16),
        vmem((nx * nc, 4, 2, rows // 2, feat), BF16),
        vmem((owners, 4, 2, rows // 2, feat), BF16),
        vmem((steps, total, chunk * tile_rows), BF16),
        vmem((total, feat), F32),
        vmem((total, feat), BF16),
        vmem((total, feat), BF16),
        vmem((total, feat), BF16),
        vmem((blocks, rows, feat), BF16),
        vmem((blocks, rows, feat), BF16),
        vmem((chunk, 4, 2, rows // 2, feat), F32),
        vmem((owners, 2, rows // 2, feat), BF16),
        vmem((owners, 2, rows // 2, feat), BF16),
        vmem((owners, 2, 2, rows // 2, feat), BF16),
        vmem((owners, 2, 2, rows // 2, feat), BF16),
        vmem((owners, 2, rows // 2, feat), BF16),
        vmem((owners, 2, rows // 2, feat), BF16),
        vmem((pieces, *piece), F32),
        vmem((nx * nz, *piece), F32),
        vmem((nx, nz, *piece), F32),
        vmem((nz, *piece), F32),
        vmem(piece, F32),
        vmem((4, *piece), F32),
        vmem((nz, *piece), F32),
        vmem((nx, nz, *piece), F32),
        vmem((nc, nx, nz, *piece), F32),
        sem((3,)),
        sem((3,)),
        sem,
        sem((steps,)),
        sem,
        sem,
        sem,
        sem((steps,)),
        sem,
        sem((steps,)),
        sem,
        sem((steps,)),
        sem,
        sem((steps,)),
        sem,
        sem((steps,)),
        sem,
        sem,
        sem,
        sem,
        sem,
        sem,
        sem,
        sem((4,)),
        sem,
        sem((nz,)),
        sem,
        sem((nx,)),
        sem,
        sem,
    ]
    smem = pl.BlockSpec(memory_space=pltpu.SMEM)
    hbm = pl.BlockSpec(memory_space=pl.ANY)
    whole = pl.BlockSpec(memory_space=pltpu.VMEM)
    hid, fg, grad = pl.pallas_call(
        functools.partial(exchange_kernel, SPLIT, chunk, scale),
        out_shape=(
            jax.ShapeDtypeStruct((blocks, rows, feat), BF16),
            jax.ShapeDtypeStruct((blocks, rows, feat), BF16),
            jax.ShapeDtypeStruct((nc, nx, nz, *piece), F32),
        ),
        in_specs=[smem, smem, hbm, hbm, whole, whole, whole, hbm],
        out_specs=(hbm, hbm, hbm),
        scratch_shapes=scratch,
        compiler_params=pltpu.CompilerParams(
            collective_id=0, has_side_effects=True, vmem_limit_bytes=60 << 20
        ),
    )(
        requests[0],
        inverse,
        feats.reshape(blocks, replicas, 2, rows // 2, feat),
        tile_vals[0],
        w_self,
        w_neigh,
        bias.reshape(1, feat),
        cotangent,
    )
    hidden, grad_self, grad_neigh, grad_bias, feat_grad = pl.pallas_call(
        finish_kernel,
        out_shape=(
            jax.ShapeDtypeStruct((blocks, rows, feat), BF16),
            jax.ShapeDtypeStruct((feat, feat), F32),
            jax.ShapeDtypeStruct((feat, feat), F32),
            jax.ShapeDtypeStruct((1, feat), F32),
            jax.ShapeDtypeStruct((blocks, rows, feat), BF16),
        ),
        in_specs=[whole, whole, whole],
        out_specs=(whole, whole, whole, whole, whole),
    )(grad.reshape(pieces, *piece), hid, fg)
    return (hidden, grad_self, grad_neigh, grad_bias.reshape(feat), feat_grad)


def solution(mesh):
    in_specs = (
        P("blk", None, None),
        P("blk", None),
        P("blk", None),
        P("blk", None),
        P("blk", None, "rep", None),
        P(),
        P(),
        P(),
        P("blk", "rep", None),
    )
    out_specs = (P("blk", "rep", None), P(), P(), P(), P("blk", "rep", None))
    return jax.shard_map(
        on_device, mesh=mesh, in_specs=in_specs, out_specs=out_specs, check_vma=False
    )
```

```python
import functools
import math

import jax
import jax.numpy as jnp
from jax import lax
from jax.experimental import pallas as pl
from jax.experimental.pallas import tpu as pltpu
from jax.sharding import PartitionSpec as P

SPLIT = (4, 8, 2)
CHUNK = 4
LAG = 7
HOP1, HOP2 = 2, 4

GRADS_AT, GRADS_GAP = 1, 3

MESH = pl.DeviceIdType.MESH
F32 = jnp.float32
BF16 = jnp.bfloat16


def exchange_kernel(
    split,
    chunk,
    scale,
    req_ref,
    inv_ref,
    feats_ref,
    tiles_ref,
    ws_ref,
    wn_ref,
    bias_ref,
    ct_ref,
    hid_out,
    fg_out,
    grad_out,
    fv,
    ct,
    tv,
    stage,
    stage_near,
    src,
    tden,
    acc,
    gp,
    agg,
    back,
    hid,
    fg,
    cf,
    r1s,
    r1r,
    r2s,
    r2r,
    r3s,
    arr,
    g_all,
    g_core,
    g_xs,
    g_zs,
    g_piece,
    g_ys,
    g_fz,
    g_fx,
    g_fc,
    in_sem,
    out_sem,
    a_send,
    a_recv,
    near_send,
    near_recv,
    b1_send,
    b1_recv,
    b2_send,
    b2_recv,
    r1_send,
    r1_recv,
    r2_send,
    r2_recv,
    r3_send,
    r3_recv,
    gc_send,
    gc_recv,
    gx_send,
    gx_recv,
    gz_send,
    gz_recv,
    gy_send,
    gy_recv,
    hz_send,
    hz_recv,
    hx_send,
    hx_recv,
    hc_send,
    hc_recv,
):
    nx, nz, nc = split
    slots = nx * nz * nc
    steps = slots // chunk
    near = nx * nc
    skip = near // chunk
    y = lax.axis_index("rep")
    b = lax.axis_index("blk")
    x = lax.div(b, nz * nc)
    z = lax.rem(lax.div(b, nc), nz)
    c = lax.rem(b, nc)
    up = lax.rem(y + 1, 4)
    down = lax.rem(y + 3, 4)
    far = lax.rem(y + 2, 4)

    def shift(s):
        dc = lax.rem(s, nc)
        p = lax.div(s, nc)
        dx = lax.rem(p, nx)
        q = lax.div(p, nx)
        dz = lax.div(q + 1, 2) * (2 * lax.rem(q, 2) - 1)
        return dx, dz, dc

    def at(px, pz, pc):
        return (px * nz + pz) * nc + pc

    def reader(s):
        dx, dz, dc = shift(s)
        return at(lax.rem(x + dx, nx), lax.rem(z + dz + nz, nz), lax.rem(c + dc, nc))

    def owner(s):
        dx, dz, dc = shift(s)
        return at(
            lax.rem(x - dx + nx, nx), lax.rem(z - dz + nz, nz), lax.rem(c - dc + nc, nc)
        )

    def remote(source, target, send, recv, rep, blk):
        return pltpu.make_async_remote_copy(
            src_ref=source,
            dst_ref=target,
            send_sem=send,
            recv_sem=recv,
            device_id=(rep, blk),
            device_id_type=MESH,
        )

    load_own = pltpu.make_async_copy(feats_ref, fv, in_sem.at[0])
    load_tiles = pltpu.make_async_copy(
        tiles_ref, tv.at[pl.ds(0, tiles_ref.shape[0])], in_sem.at[1]
    )
    load_ct = pltpu.make_async_copy(ct_ref, ct, in_sem.at[2])
    load_own.start()
    load_tiles.start()
    load_ct.start()

    barrier = pltpu.get_barrier_semaphore()

    def greet(s, carry):
        pl.semaphore_signal(barrier, inc=1, device_id=(y, reader(s)), device_id_type=MESH)
        return carry

    lax.fori_loop(1, slots, greet, 0)
    for d in range(1, 4):
        pl.semaphore_signal(
            barrier, inc=1, device_id=(lax.rem(y + d, 4), b), device_id_type=MESH
        )
    tv[tiles_ref.shape[0]] = jnp.zeros(tv.shape[1:], BF16)
    load_own.wait()

    def gather(s, carry):
        stage[s] = fv[req_ref[reader(s)], y]
        return carry

    lax.fori_loop(near, slots, gather, 0)

    def gather_near(s, carry):
        stage_near[s] = fv[req_ref[reader(s)]]
        return carry

    lax.fori_loop(1, near, gather_near, 0)
    src[0] = fv[req_ref[b]]
    acc[...] = jnp.zeros_like(acc)
    blocks = fv.shape[0]
    rows = fv.shape[2] * fv.shape[3]
    width = 4 * rows
    feat = fv.shape[-1]
    total = blocks * rows
    load_tiles.wait()

    def spread(i, carry):
        for k in range(chunk):
            o = owner(i * chunk + k)
            for d in range(blocks):
                tden[i, pl.ds(d * rows, rows), pl.ds(k * width, width)] = tv[
                    inv_ref[d * slots + o]
                ]
        return carry

    lax.fori_loop(0, steps, spread, 0)
    pl.semaphore_wait(barrier, slots - 1 + 3)

    def a_copy(s):
        return remote(
            stage.at[s], src.at[s, y], a_send, a_recv.at[lax.div(s, chunk)], y, reader(s)
        )

    def a_start(s, carry):
        a_copy(s).start()
        return carry

    lax.fori_loop(near, slots, a_start, 0)

    def near_start(s, carry):
        remote(stage_near.at[s], src.at[s], near_send, near_recv, y, reader(s)).start()
        return carry

    lax.fori_loop(1, near, near_start, 0)

    def wait_recv(target, recv):
        remote(target, target, in_sem.at[0], recv, up, b).wait_recv()

    def wait_send(source, send):
        remote(source, source, send, in_sem.at[0], up, b).wait_send()

    def b1_copy(i, d):
        part = src.at[pl.ds(i * chunk, chunk), y]
        return remote(part, part, b1_send, b1_recv.at[i], (up, down)[d], b)

    def b2_copy(i, d):
        part = src.at[pl.ds(i * chunk, chunk), (down, up)[d], d]
        return remote(part, part, b2_send, b2_recv.at[i], (up, down)[d], b)

    def mix(i):
        blockset = src[pl.ds(i * chunk, chunk)].reshape(chunk * width, feat)
        acc[...] += jnp.dot(tden[i], blockset, preferred_element_type=F32)

    def forward(i, carry):
        @pl.when(i < steps)
        def _():
            wait_recv(src.at[pl.ds(i * chunk, chunk), y], a_recv.at[i])
            for d in range(2):
                b1_copy(i, d).start()

        @pl.when(jnp.logical_and(i >= skip + HOP1, i < steps + HOP1))
        def _():
            wait_recv(src.at[pl.ds((i - HOP1) * chunk, chunk), pl.ds(0, 2)], b1_recv.at[i - HOP1])
            for d in range(2):
                b2_copy(i - HOP1, d).start()

        @pl.when(i >= skip + HOP2)
        def _():
            wait_recv(src.at[pl.ds((i - HOP2) * chunk, chunk), far], b2_recv.at[i - HOP2])
            mix(i - HOP2)

        @pl.when(i == steps // 2)
        def _():
            wait_recv(src.at[pl.ds(1, near - 1)], near_recv)
            for n in range(skip):
                mix(n)

        return carry

    lax.fori_loop(skip, steps + HOP2, forward, 0)

    load_ct.wait()
    part = total // 4
    per = blocks // 4

    def dense(n, carry):
        here = pl.ds(n * part, part)
        blk = pl.ds(n * per, per)
        mine = fv[blk, y].reshape(part, feat)
        mixed = acc[here, :].astype(BF16)
        agg[here, :] = mixed
        pre = jnp.dot(mine, ws_ref[...], preferred_element_type=F32)
        pre = pre + jnp.dot(mixed, wn_ref[...], preferred_element_type=F32) + bias_ref[...]
        gate = 1.0 / (1.0 + jnp.exp(-pre))
        hid[blk] = (pre * gate).astype(BF16).reshape(per, rows, feat)
        down_grad = ct[blk].reshape(part, feat).astype(F32)
        grad = (down_grad * gate * (1.0 + pre * (1.0 - gate))).astype(BF16)
        gp[here, :] = grad
        back[here, :] = lax.dot_general(
            grad, wn_ref[...], (((1,), (1,)), ((), ())), preferred_element_type=F32
        ).astype(BF16)
        return carry

    lax.fori_loop(0, 4, dense, 0)
    save_hid = pltpu.make_async_copy(hid, hid_out, out_sem.at[0])
    save_hid.start()

    def r1_copy(j, d):
        here = pl.ds(j * chunk, chunk)
        return remote(
            r1s.at[here, d],
            r1r.at[here, d],
            r1_send,
            r1_recv.at[j],
            (up, down)[d],
            b,
        )

    def r2_copy(j, d):
        here = pl.ds(j * chunk, chunk)
        return remote(
            r2s.at[here, d],
            r2r.at[here, d],
            r2_send,
            r2_recv.at[j],
            (up, down)[d],
            b,
        )

    def r3_copy(s):
        return remote(
            r3s.at[s], arr.at[s], r3_send, r3_recv.at[lax.div(s, chunk)], y, owner(s)
        )

    half = nx * nz
    other = at(x, z, nc - 1 - c) if nc == 2 else b

    def core_copy():
        return remote(
            g_all.at[pl.ds((1 - c) * half, half)], g_core, gc_send, gc_recv, y, other
        )

    def x_copy(d):
        peer = lax.rem(x + d, nx)
        return remote(
            g_all.at[pl.ds(c * half + peer * nz, nz)],
            g_xs.at[d],
            gx_send,
            gx_recv,
            y,
            at(peer, z, c),
        )

    def z_copy(d):
        peer = lax.rem(z + d, nz)
        return remote(
            g_all.at[c * half + x * nz + peer],
            g_zs.at[d],
            gz_send,
            gz_recv,
            y,
            at(x, peer, c),
        )

    def y_copy(d):
        return remote(
            g_piece, g_ys.at[y], gy_send, gy_recv.at[d], lax.rem(y + d, 4), b
        )

    def zz_copy(d):
        return remote(
            g_fz.at[z],
            g_fz.at[z],
            hz_send,
            hz_recv.at[d],
            y,
            at(x, lax.rem(z + d, nz), c),
        )

    def xx_copy(d):
        return remote(
            g_fz, g_fx.at[x], hx_send, hx_recv.at[d], y, at(lax.rem(x + d, nx), z, c)
        )

    def cc_copy():
        return remote(g_fx, g_fc.at[c], hc_send, hc_recv, y, other)

    def grads():
        feat_rows = fv[:, y].reshape(total, feat)
        grad = gp[...]
        first = lax.dot_general(
            feat_rows, grad, (((0,), (0,)), ((), ())), preferred_element_type=F32
        )
        second = lax.dot_general(
            agg[...], grad, (((0,), (0,)), ((), ())), preferred_element_type=F32
        )
        pieces = nc * half
        tall = 2 * feat // pieces
        g_all[:, :, pl.ds(feat, 128)] = jnp.zeros((pieces, tall, 128), F32)
        g_all[pl.ds(0, pieces // 2), :, pl.ds(0, feat)] = (first * scale).reshape(
            pieces // 2, tall, feat
        )
        g_all[pl.ds(pieces // 2, pieces // 2), :, pl.ds(0, feat)] = (second * scale).reshape(
            pieces // 2, tall, feat
        )
        down_sum = jnp.sum(grad.astype(F32), axis=0, keepdims=True) * scale
        for n in range(feat // 128):
            g_all[0, pl.ds(n, 1), pl.ds(feat, 128)] = down_sum[:, n * 128 : (n + 1) * 128]
        if nc == 2:
            core_copy().start()

    def grads_core():
        if nc == 2:
            core_copy().wait_recv()
            here = pl.ds(c * half, half)
            g_all[here] = g_all[here] + g_core[...]
        for d in range(1, nx):
            x_copy(d).start()

    def grads_x():
        here = pl.ds(c * half + x * nz, nz)
        value = g_all[here]
        wait_recv(g_xs.at[pl.ds(1, nx - 1)], gx_recv)
        for d in range(1, nx):
            value = value + g_xs[d]
        g_all[here] = value
        for d in range(1, nz):
            z_copy(d).start()

    def grads_z():
        value = g_all[c * half + x * nz + z]
        wait_recv(g_zs.at[pl.ds(1, nz - 1)], gz_recv)
        for d in range(1, nz):
            value = value + g_zs[d]
        g_piece[...] = value
        g_ys[y] = value
        for d in range(1, 4):
            y_copy(d).start()

    def grads_y():
        for d in range(1, 4):
            source = lax.rem(y + 4 - d, 4)
            wait_recv(g_ys.at[source], gy_recv.at[d])
        g_fz[z] = (g_ys[0] + g_ys[1]) + (g_ys[2] + g_ys[3])
        for d in range(1, nz):
            zz_copy(d).start()

    def grads_zz():
        for d in range(1, nz):
            source = lax.rem(z + nz - d, nz)
            wait_recv(g_fz.at[source], hz_recv.at[d])
        g_fx[x] = g_fz[...]
        for d in range(1, nx):
            xx_copy(d).start()

    def grads_xx():
        for d in range(1, nx):
            source = lax.rem(x + nx - d, nx)
            wait_recv(g_fx.at[source], hx_recv.at[d])
        g_fc[c] = g_fx[...]
        if nc == 2:
            cc_copy().start()

    def grads_cc():
        if nc == 2:
            wait_recv(g_fc.at[1 - c], hc_recv)

    def collect(j):
        lane = lax.broadcasted_iota(jnp.int32, (1, chunk * rows), 1)
        target = lax.rem(lane, rows)
        for k in range(chunk):
            s = j * chunk + k
            inside = jnp.logical_and(lane >= k * rows, lane < (k + 1) * rows)
            target = target + jnp.where(inside, req_ref[reader(s)] * rows, 0)

        @pl.when(j > 0)
        def _():
            wait_recv(arr.at[pl.ds(j * chunk, chunk)], r3_recv.at[j])

        @pl.when(j == 0)
        def _():
            wait_recv(arr.at[pl.ds(1, chunk - 1)], r3_recv.at[0])

        row = lax.broadcasted_iota(jnp.int32, (total, chunk * rows), 0)
        pick = jnp.where(row == target, 1.0, 0.0).astype(BF16)
        came = arr[pl.ds(j * chunk, chunk)].reshape(chunk * rows, feat)
        acc[...] += jnp.dot(pick, came, preferred_element_type=F32)

    stages = (grads_core, grads_x, grads_z, grads_y, grads_zz, grads_xx)

    def turn(i):
        n = lax.div(i, skip)
        odd = lax.rem(n, 2)
        early = nz - 1 - lax.div(n, 2)
        late = lax.rem(lax.div(n + 1, 2), nz // 2)
        return ((1 - odd) * early + odd * late) * skip + lax.rem(i, skip)

    def backward(i, carry):

        @pl.when(i < steps)
        def _():
            j = turn(i)
            product = lax.dot_general(
                tden[j], back[...], (((0,), (0,)), ((), ())), preferred_element_type=F32
            )
            here = pl.ds(j * chunk, chunk)
            cf[...] = product.reshape(chunk, 4, 2, rows // 2, feat)
            r1s[here] = cf[:, far].astype(BF16)
            r2s[here, 0] = cf[:, up].astype(BF16)
            r2s[here, 1] = cf[:, down].astype(BF16)
            r3s[here] = cf[:, y].astype(BF16)
            for d in range(2):
                r1_copy(j, d).start()

        @pl.when(jnp.logical_and(i >= HOP1, i < steps + HOP1))
        def _():
            n = turn(i - HOP1)
            here = pl.ds(n * chunk, chunk)
            wait_recv(r1r.at[here], r1_recv.at[n])
            for d in range(2):
                r2s[here, d, d] = (
                    r2s[here, d, d].astype(F32) + r1r[here, d].astype(F32)
                ).astype(BF16)
            for d in range(2):
                r2_copy(n, d).start()

        @pl.when(jnp.logical_and(i >= HOP2, i < steps + HOP2))
        def _():
            n = turn(i - HOP2)
            here = pl.ds(n * chunk, chunk)
            wait_recv(r2r.at[here], r2_recv.at[n])
            r3s[here] = (
                r3s[here].astype(F32) + r2r[here, 0].astype(F32) + r2r[here, 1].astype(F32)
            ).astype(BF16)
            for k in range(chunk):
                s = n * chunk + k

                @pl.when(s > 0)
                def _():
                    r3_copy(s).start()

                @pl.when(s == 0)
                def _():
                    arr[0] = r3s[0]

        @pl.when(i == GRADS_AT)
        def _():
            grads()

        @pl.when(i == GRADS_AT - 1)
        def _():
            grad = gp[...]
            acc[...] = lax.dot_general(
                grad, ws_ref[...], (((1,), (1,)), ((), ())), preferred_element_type=F32
            )

        for n, stage_fn in enumerate(stages):

            @pl.when(i == min(GRADS_AT + GRADS_GAP * (n + 1), steps + HOP2 - 1))
            def _(stage_fn=stage_fn):
                stage_fn()

        @pl.when(i >= HOP2 + LAG)
        def _():
            collect(turn(i - HOP2 - LAG))

        return carry

    lax.fori_loop(0, steps + HOP2, backward, 0)
    for n in range(LAG):
        collect(turn(jnp.int32(steps - LAG + n)))
    fg[...] = acc[...].astype(BF16).reshape(fg.shape)
    save_fg = pltpu.make_async_copy(fg, fg_out, out_sem.at[1])
    save_fg.start()
    grads_cc()
    save_grad = pltpu.make_async_copy(g_fc, grad_out, out_sem.at[2])
    save_grad.start()

    wait_send(stage.at[pl.ds(near, slots - near)], a_send)
    wait_send(stage_near.at[pl.ds(1, near - 1)], near_send)
    wait_send(src.at[pl.ds(near, slots - near), pl.ds(0, 2)], b1_send)
    wait_send(src.at[pl.ds(near, slots - near), 0], b2_send)
    wait_send(r1s, r1_send)
    wait_send(r2s, r2_send)
    wait_send(r3s.at[pl.ds(1, slots - 1)], r3_send)
    if nc == 2:
        core_copy().wait_send()
        cc_copy().wait_send()
    wait_send(g_xs.at[pl.ds(1, nx - 1)], gx_send)
    wait_send(g_zs.at[pl.ds(1, nz - 1)], gz_send)
    wait_send(g_ys.at[pl.ds(0, 3)], gy_send)
    wait_send(g_fz.at[pl.ds(0, nz - 1)], hz_send)
    wait_send(g_fx.at[pl.ds(0, nx - 1)], hx_send)
    save_hid.wait()
    save_fg.wait()
    save_grad.wait()


def finish_kernel(grad_ref, hid_ref, fg_ref, hid_o, gs_o, gn_o, gb_o, fg_o):
    pieces = grad_ref.shape[0]
    feat = gs_o.shape[0]
    gs_o[...] = grad_ref[pl.ds(0, pieces // 2), :, pl.ds(0, feat)].reshape(feat, feat)
    gn_o[...] = grad_ref[pl.ds(pieces // 2, pieces // 2), :, pl.ds(0, feat)].reshape(feat, feat)
    for n in range(feat // 128):
        gb_o[:, pl.ds(n * 128, 128)] = grad_ref[0, pl.ds(n, 1), pl.ds(feat, 128)]
    hid_o[...] = hid_ref[...]
    fg_o[...] = fg_ref[...]


def on_device(feats, requests, tile_dest, tile_slot, tile_vals, w_self, w_neigh, bias, cotangent):
    owners = lax.axis_size("blk")
    replicas = lax.axis_size("rep")
    nx, nz, nc = SPLIT
    chunk = CHUNK
    steps = owners // chunk
    blocks, tile_rows, feat = feats.shape
    rows = tile_rows // replicas
    total = blocks * rows
    tiles = tile_vals.shape[1]
    pieces = nc * nx * nz
    tall = 2 * feat // pieces
    scale = 1.0 / math.sqrt(owners * blocks * tile_rows)

    number = jnp.arange(tiles, dtype=jnp.int32)
    code = tile_dest[0] * owners + tile_slot[0]
    place = jnp.arange(blocks * owners, dtype=jnp.int32)
    inverse = tiles + jnp.sum(
        jnp.where(code[None, :] == place[:, None], number[None, :] - tiles, 0), axis=-1
    )

    vmem = pltpu.VMEM
    sem = pltpu.SemaphoreType.DMA
    piece = (tall, feat + 128)
    scratch = [
        vmem((blocks, 4, 2, rows // 2, feat), BF16),
        vmem((blocks, rows, feat), BF16),
        vmem((tiles + 1, rows, tile_rows), BF16),
        vmem((owners, 2, rows // 2, feat), BF16),
        vmem((nx * nc, 4, 2, rows // 2, feat), BF16),
        vmem((owners, 4, 2, rows // 2, feat), BF16),
        vmem((steps, total, chunk * tile_rows), BF16),
        vmem((total, feat), F32),
        vmem((total, feat), BF16),
        vmem((total, feat), BF16),
        vmem((total, feat), BF16),
        vmem((blocks, rows, feat), BF16),
        vmem((blocks, rows, feat), BF16),
        vmem((chunk, 4, 2, rows // 2, feat), F32),
        vmem((owners, 2, rows // 2, feat), BF16),
        vmem((owners, 2, rows // 2, feat), BF16),
        vmem((owners, 2, 2, rows // 2, feat), BF16),
        vmem((owners, 2, 2, rows // 2, feat), BF16),
        vmem((owners, 2, rows // 2, feat), BF16),
        vmem((owners, 2, rows // 2, feat), BF16),
        vmem((pieces, *piece), F32),
        vmem((nx * nz, *piece), F32),
        vmem((nx, nz, *piece), F32),
        vmem((nz, *piece), F32),
        vmem(piece, F32),
        vmem((4, *piece), F32),
        vmem((nz, *piece), F32),
        vmem((nx, nz, *piece), F32),
        vmem((nc, nx, nz, *piece), F32),
        sem((3,)),
        sem((3,)),
        sem,
        sem((steps,)),
        sem,
        sem,
        sem,
        sem((steps,)),
        sem,
        sem((steps,)),
        sem,
        sem((steps,)),
        sem,
        sem((steps,)),
        sem,
        sem((steps,)),
        sem,
        sem,
        sem,
        sem,
        sem,
        sem,
        sem,
        sem((4,)),
        sem,
        sem((nz,)),
        sem,
        sem((nx,)),
        sem,
        sem,
    ]
    smem = pl.BlockSpec(memory_space=pltpu.SMEM)
    hbm = pl.BlockSpec(memory_space=pl.ANY)
    whole = pl.BlockSpec(memory_space=pltpu.VMEM)
    hid, fg, grad = pl.pallas_call(
        functools.partial(exchange_kernel, SPLIT, chunk, scale),
        out_shape=(
            jax.ShapeDtypeStruct((blocks, rows, feat), BF16),
            jax.ShapeDtypeStruct((blocks, rows, feat), BF16),
            jax.ShapeDtypeStruct((nc, nx, nz, *piece), F32),
        ),
        in_specs=[smem, smem, hbm, hbm, whole, whole, whole, hbm],
        out_specs=(hbm, hbm, hbm),
        scratch_shapes=scratch,
        compiler_params=pltpu.CompilerParams(
            collective_id=0, has_side_effects=True, vmem_limit_bytes=60 << 20
        ),
    )(
        requests[0],
        inverse,
        feats.reshape(blocks, replicas, 2, rows // 2, feat),
        tile_vals[0],
        w_self,
        w_neigh,
        bias.reshape(1, feat),
        cotangent,
    )
    hidden, grad_self, grad_neigh, grad_bias, feat_grad = pl.pallas_call(
        finish_kernel,
        out_shape=(
            jax.ShapeDtypeStruct((blocks, rows, feat), BF16),
            jax.ShapeDtypeStruct((feat, feat), F32),
            jax.ShapeDtypeStruct((feat, feat), F32),
            jax.ShapeDtypeStruct((1, feat), F32),
            jax.ShapeDtypeStruct((blocks, rows, feat), BF16),
        ),
        in_specs=[whole, whole, whole],
        out_specs=(whole, whole, whole, whole, whole),
    )(grad.reshape(pieces, *piece), hid, fg)
    return (hidden, grad_self, grad_neigh, grad_bias.reshape(feat), feat_grad)


def solution(mesh):
    in_specs = (
        P("blk", None, None),
        P("blk", None),
        P("blk", None),
        P("blk", None),
        P("blk", None, "rep", None),
        P(),
        P(),
        P(),
        P("blk", "rep", None),
    )
    out_specs = (P("blk", "rep", None), P(), P(), P(), P("blk", "rep", None))
    return jax.shard_map(
        on_device, mesh=mesh, in_specs=in_specs, out_specs=out_specs, check_vma=False
    )
```
